32 devices in a mesh: member: 2 (over x), dom: 16 (over z, y, core).
Axes of the slice: x: 2, y: 2, z: 4, core: 2. Of those that a mesh axis runs over, the one named last changes fastest.
Arguments:
- atom_feat: bfloat16 [128, 4096], P('member', 'dom'), parts along dimension 0, may hold values from -6 to 6
- bond_feat: bfloat16 [128, 32768], P('member', 'dom'), parts along dimension 0, may hold values from -6 to 6
- angle_feat: bfloat16 [128, 32768], P('member', 'dom'), parts along dimension 0, may hold values from -6 to 6
- atom_cot: bfloat16 [128, 4096], P('member', 'dom'), parts along dimension 0, may hold values from -6 to 6
- bond_cot: bfloat16 [128, 32768], P('member', 'dom'), parts along dimension 0, may hold values from -6 to 6
- angle_weight: bfloat16 [256, 256], P('member'), parts along dimension 0, may hold values from -0.375 to 0.375
- bond_weight: bfloat16 [128, 64], P('member'), parts along dimension 0, may hold values from -0.75 to 0.75
- message_weight: bfloat16 [256, 192], P('member'), parts along dimension 0, may hold values from -0.4375 to 0.4375
- out_weight: bfloat16 [128, 64], P('member'), parts along dimension 0, may hold values from -0.75 to 0.75
- send_list: int32 [16, 128], P('dom'), may hold values from 0 to 255
- bond_src: int32 [32768], P('dom'), may hold values from 0 to 383
- bond_dst: int32 [32768], P('dom'), may hold values from 0 to 383
- bond_count: int32 [16], replicated, may hold values from 1 to 2048, 13107 in all
- angle_first: int32 [32768], P('dom'), may hold values from 0 to 2047
- angle_second: int32 [32768], P('dom'), may hold values from 0 to 2047
- angle_count: int32 [16], replicated, may hold values from 1 to 2048, 13107 in all
Outputs:
- new_atom: bfloat16 [128, 4096], P('member', 'dom'), parts along dimension 0
- new_bond: bfloat16 [128, 32768], P('member', 'dom'), parts along dimension 0
- grad_atom: bfloat16 [128, 4096], P('member', 'dom'), parts along dimension 0
- grad_bond: bfloat16 [128, 32768], P('member', 'dom'), parts along dimension 0
The draws below stay inside these ranges and needn't reach their ends.
There are 2 independent parts, one for each index of `member`. The reference program is written for one: setup_inputs(seed, part) draws one part's arguments, and reference() takes and returns one part's arrays. A program takes and returns all parts, laid end to end along the dimension named above; an argument that names none is the same for every part. Nothing has to cross between parts.
Inputs may be any that keep to these rules, and one draw needn't show every extreme that they name: `send_list`: indices into the listing partition's own atoms. `bond_src`: rows below 256 are the partition's own atoms, the others listed rows of partitions. `bond_dst`: same row space as bond_src. `bond_count`: live slots come first in each partition. `angle_count`: live slots come first in each partition.
All inputs are finite; a program needn't handle non-finite values.
Results may differ from the reference program's by a relative error of at most 0.0065.
Values may be sent and summed in bfloat16 or wider, within the bound.
A program may use at most 64 MiB of HBM per device.

```python
import math
import jax
import jax.numpy as jnp
import numpy as np
from jax import lax

F = 64
A_DEV = 256
B_DEV = 2048
G_DEV = 2048
SLOT = 8
ATOMS = 4096
BONDS = 32768
ANGLES = 32768
RECV = 128
ROWSPACE = 384
BOND_LIVE = 13107
ANGLE_LIVE = 13107
N_DOM = 16


def place_ends(result, stream_key, low, high):
    dims = result.shape
    place = [jax.random.randint(jax.random.fold_in(stream_key, axis), (), 0, dims[axis]) for axis in range(len(dims))]
    result = result.at[tuple(place)].set(low)
    longest = dims.index(max(dims))
    place[longest] = (place[longest] + 1) % dims[longest]
    return result.at[tuple(place)].set(high)


def levels(key, dims, split, least, top_value):
    def one(position, shards_of):
        steps = jax.random.uniform(jax.random.fold_in(jax.random.fold_in(key, 6), position), (shards_of,), jnp.float32, least / len(split), top_value / len(split))
        return jnp.repeat(jnp.exp(steps), dims[position] // shards_of).reshape((-1,) + (1,) * (len(dims) - position - 1))

    factor_of = one(*split[0])
    for cut in split[1:]:
        factor_of = factor_of * one(*cut)
    return factor_of


def length_profile(number_of, total, most, lean):
    weights = [(1 << 20) // math.isqrt(grade ** lean) + 1 for grade in range(2, number_of + 1)]
    surplus, holding = total - most - (number_of - 1), [1] * (number_of - 1)
    while surplus > 0:
        candidates = [i for i in range(number_of - 1) if holding[i] < most]
        mass, remaining = sum([weights[i] for i in candidates]), surplus
        for i in candidates:
            more = min(most - holding[i], max(1, remaining * weights[i] // mass), surplus)
            holding[i] = holding[i] + more
            surplus = surplus - more
    return np.array([most] + holding)


def ragged(own_key, amount, total, bound, lean):
    if amount == 2:
        one = jax.random.randint(own_key, (), max(1, total - bound), min(bound, total - 1) + 1)
        return jnp.stack([one, total - one])
    sizes = jnp.asarray(length_profile(amount, total, bound, lean), jnp.int32)
    pairs = (amount - 1) // 2
    donor, receiver = sizes[1:1 + 2 * pairs:2], sizes[2:2 + 2 * pairs:2]
    margin = jnp.minimum(donor - 1, bound - receiver)
    shifted = jax.random.randint(jax.random.fold_in(own_key, 1), (pairs,), 0, 1 << 20) % (margin + 1)
    sizes = sizes.at[1:1 + 2 * pairs:2].set(donor - shifted).at[2:2 + 2 * pairs:2].set(receiver + shifted)
    return sizes[jax.random.permutation(jax.random.fold_in(own_key, 2), amount)]


def noise(stream_key, shape, scale, reach, cuts=(), kind=jnp.bfloat16):
    values = jax.random.normal(stream_key, shape, jnp.float32) * scale
    if len(cuts) > 0:
        values = levels(stream_key, shape, cuts, -0.22, 0.18) * values
    return jnp.clip(values, min=-reach, max=reach).astype(kind)


def setup_inputs(seed: int = 0, part: int = 0) -> dict:
    seeds = jax.random.split(jax.random.key(seed), 17)
    part_keys = jax.random.split(jax.random.fold_in(seeds[16], part), 17)
    return {
        "atom_feat": noise(part_keys[0], (F, ATOMS), 1.0, 6.0, ((1, 16),)),
        "bond_feat": noise(part_keys[1], (F, BONDS), 1.0, 6.0, ((1, 16),)),
        "angle_feat": noise(part_keys[2], (F, ANGLES), 1.0, 6.0, ((1, 16),)),
        "atom_cot": noise(part_keys[3], (F, ATOMS), 1.0, 6.0, ((1, 16),)),
        "bond_cot": noise(part_keys[4], (F, BONDS), 1.0, 6.0, ((1, 16),)),
        "angle_weight": noise(part_keys[5], (2 * F, 4 * F), (4 * F) ** -0.5, 0.375),
        "bond_weight": noise(part_keys[6], (F, F), F ** -0.5, 0.75),
        "message_weight": noise(part_keys[7], (2 * F, 3 * F), (3 * F) ** -0.5, 0.4375),
        "out_weight": noise(part_keys[8], (F, F), F ** -0.5, 0.75),
        "send_list": place_ends(jax.random.randint(seeds[9], (N_DOM, RECV), 0, A_DEV), jax.random.fold_in(seeds[9], 1), 0, A_DEV - 1).astype(jnp.int32),
        "bond_src": place_ends(jax.random.randint(seeds[10], (BONDS,), 0, ROWSPACE), jax.random.fold_in(seeds[10], 1), 0, ROWSPACE - 1).astype(jnp.int32),
        "bond_dst": place_ends(jax.random.randint(seeds[11], (BONDS,), 0, ROWSPACE), jax.random.fold_in(seeds[11], 1), 0, ROWSPACE - 1).astype(jnp.int32),
        "bond_count": ragged(seeds[12], N_DOM, BOND_LIVE, B_DEV, 2).astype(jnp.int32),
        "angle_first": place_ends(jax.random.randint(seeds[13], (ANGLES,), 0, B_DEV), jax.random.fold_in(seeds[13], 1), 0, B_DEV - 1).astype(jnp.int32),
        "angle_second": place_ends(jax.random.randint(seeds[14], (ANGLES,), 0, B_DEV), jax.random.fold_in(seeds[14], 1), 0, B_DEV - 1).astype(jnp.int32),
        "angle_count": ragged(seeds[15], N_DOM, ANGLE_LIVE, G_DEV, 2).astype(jnp.int32),
    }


def gate(value):
    half = value.shape[0] // 2
    first = value[:half]
    return first * jax.nn.sigmoid(first) * jax.nn.sigmoid(value[half:])


def gate_back(value, upstream):
    half = value.shape[0] // 2
    first = value[:half]
    second = value[half:]
    sig_a = jax.nn.sigmoid(first)
    sig_c = jax.nn.sigmoid(second)
    part_a = upstream * sig_c * sig_a * (1.0 + first * (1.0 - sig_a))
    part_c = upstream * first * sig_a * sig_c * (1.0 - sig_c)
    return jnp.concatenate([part_a, part_c], 0)


def rounded(value):
    return lax.optimization_barrier(value.astype(jnp.bfloat16)).astype(jnp.float32)


def reference(atom_feat, bond_feat, angle_feat, atom_cot, bond_cot, angle_weight, bond_weight, message_weight, out_weight, send_list, bond_src, bond_dst, bond_count, angle_first, angle_second, angle_count):
    bond_ids = jnp.arange(BONDS, dtype=jnp.int32)
    owner = (bond_ids // B_DEV).astype(jnp.int32)

    def resolve(index):
        local = index < A_DEV
        offset = jnp.maximum(index - A_DEV, 0).astype(jnp.int32)
        sender = (offset // SLOT).astype(jnp.int32)
        slot_pos = (offset % SLOT).astype(jnp.int32)
        remote = sender * A_DEV + send_list[sender, owner * SLOT + slot_pos]
        return jnp.where(local, owner * A_DEV + index, remote).astype(jnp.int32)

    src = resolve(bond_src)
    dst = resolve(bond_dst)
    bond_live = ((bond_ids % B_DEV) < bond_count[owner]).astype(jnp.float32)
    angle_ids = jnp.arange(ANGLES, dtype=jnp.int32)
    angle_owner = (angle_ids // G_DEV).astype(jnp.int32)
    angle_live = ((angle_ids % G_DEV) < angle_count[angle_owner]).astype(jnp.float32)
    first = (angle_owner * B_DEV + angle_first).astype(jnp.int32)
    second = (angle_owner * B_DEV + angle_second).astype(jnp.int32)
    width = atom_feat.shape[0]

    src_rows = atom_feat[:, src]
    dst_rows = atom_feat[:, dst]
    inputs = jnp.concatenate([src_rows[:, first], bond_feat[:, first], bond_feat[:, second], angle_feat], 0)
    z_val = jnp.dot(angle_weight, inputs, preferred_element_type=jnp.float32)
    message = rounded(gate(z_val)) * angle_live
    summed = jnp.zeros((width, BONDS), jnp.float32).at[:, first].add(message)
    update = jnp.dot(bond_weight, summed.astype(jnp.bfloat16), preferred_element_type=jnp.float32)
    new_bond = (bond_feat.astype(jnp.float32) + bond_live * update).astype(jnp.bfloat16)
    inputs_two = jnp.concatenate([src_rows, dst_rows, new_bond], 0)
    hidden = jnp.dot(message_weight, inputs_two, preferred_element_type=jnp.float32)
    bond_message = rounded(gate(hidden)) * bond_live
    pooled = jnp.zeros((width, ATOMS), jnp.float32).at[:, dst].add(bond_message)
    new_atom = (atom_feat.astype(jnp.float32) + jnp.dot(out_weight, pooled.astype(jnp.bfloat16), preferred_element_type=jnp.float32)).astype(jnp.bfloat16)

    atom_back = jnp.dot(out_weight.T, atom_cot, preferred_element_type=jnp.float32).astype(jnp.bfloat16)
    dmessage = atom_back[:, dst].astype(jnp.float32) * bond_live
    dhidden = gate_back(hidden, dmessage).astype(jnp.bfloat16)
    back_bond = jnp.dot(message_weight.T, dhidden, preferred_element_type=jnp.float32)
    dtotal = bond_cot.astype(jnp.float32) + back_bond[2 * width:]
    dsummed = jnp.dot(bond_weight.T, (bond_live * dtotal).astype(jnp.bfloat16), preferred_element_type=jnp.float32)
    dz_val = gate_back(z_val, dsummed[:, first] * angle_live).astype(jnp.bfloat16)
    back_angle = jnp.dot(angle_weight[:, :3 * width].T, dz_val, preferred_element_type=jnp.float32)
    grad_src = back_bond[:width].at[:, first].add(back_angle[:width])
    grad_bond = dtotal.at[:, first].add(back_angle[width:2 * width]).at[:, second].add(back_angle[2 * width:]).astype(jnp.bfloat16)
    atom_terms = jnp.zeros((width, ATOMS), jnp.float32).at[:, src].add(grad_src).at[:, dst].add(back_bond[width:2 * width])
    grad_atom = (atom_cot.astype(jnp.float32) + atom_terms).astype(jnp.bfloat16)
    return new_atom, new_bond, grad_atom, grad_bond
```

```python
import functools

import jax
import jax.numpy as jnp
from jax import lax
from jax.experimental import pallas as pl
from jax.experimental.pallas import tpu as pltpu
from jax.sharding import PartitionSpec as P

F32 = jnp.float32
BF16 = jnp.bfloat16
GROUP = 256
CHUNK = 512


def dot(a, b):
    return lax.dot_general(a, b, (((1,), (0,)), ((), ())), preferred_element_type=F32)


def dot_nt(a, b):
    return lax.dot_general(a, b, (((1,), (1,)), ((), ())), preferred_element_type=F32)


def flip(a):
    return jnp.transpose(a.astype(F32)).astype(BF16)


def onehot(rows, index):
    grid = lax.broadcasted_iota(jnp.int32, (rows, index.shape[1]), 0)
    return jnp.where(grid == index, 1.0, 0.0).astype(BF16)


def wide_row(index, rows=16):
    return jnp.broadcast_to(index, (rows, index.shape[1])).astype(F32).astype(BF16)


def fill_table(table, index, cols):
    rows = table.shape[0]
    step = lax.broadcasted_iota(jnp.int32, (16, CHUNK), 0).astype(F32).astype(BF16)
    one = jnp.ones((16, CHUNK), BF16)
    zero = jnp.zeros((16, CHUNK), BF16)
    for base in range(0, rows, GROUP):
        wide = wide_row(index - base)
        for at in range(0, min(GROUP, rows - base), 16):
            table[base + at : base + at + 16, cols] = jnp.where(wide == step + at, one, zero)


def gate_parts(value):
    half = value.shape[0] // 2
    first = value[:half]
    sig_a = 0.5 * jnp.tanh(0.5 * first) + 0.5
    sig_c = 0.5 * jnp.tanh(0.5 * value[half:]) + 0.5
    prod = first * sig_a
    out = prod * sig_c
    return out, sig_c * (sig_a + prod * (1.0 - sig_a)), out * (1.0 - sig_c)


def pick_group(stacked, group, groups, width):
    acc = jnp.zeros((width, stacked.shape[1]), F32)
    group = jnp.broadcast_to(group, acc.shape)
    for k in range(groups):
        acc = jnp.where(group == k, stacked[k * width : (k + 1) * width], acc)
    return acc


def skewed(count, *stages):
    for turn in range(count + len(stages) - 1):
        for late in reversed(range(len(stages))):
            if 0 <= turn - late < count:
                stages[late](turn - late)


INPUTS = 16


def kernel(n, axis, *refs):
    sources = refs[:INPUTS]
    outs = refs[INPUTS : INPUTS + 4]
    staged = list(refs[INPUTS + 4 : 2 * INPUTS + 3])
    in_sem, zin_ref = refs[2 * INPUTS + 3 : 2 * INPUTS + 5]
    width = sources[0].shape[0]
    staged.insert(2, zin_ref.at[3 * width : 4 * width, :])
    copies = [
        pltpu.make_async_copy(sources[k], staged[k], in_sem.at[k]) for k in range(INPUTS)
    ]
    body(n, axis, copies, *staged, *outs, zin_ref, *refs[2 * INPUTS + 5 :])


def body(
    n,
    axis,
    copies,
    atom_ref,
    bond_ref,
    angle_ref,
    acot_ref,
    bcot_ref,
    wa_ref,
    wb_ref,
    wm_ref,
    wo_ref,
    list_ref,
    src_ref,
    dst_ref,
    first_ref,
    second_ref,
    bcount_ref,
    acount_ref,
    new_atom_ref,
    new_bond_ref,
    grad_atom_ref,
    grad_bond_ref,
    zin_ref,
    send_ref,
    recv_ref,
    send2_ref,
    recv2_ref,
    table_pair,
    table_source,
    table_dst,
    stack_ref,
    bin_ref,
    up_ref,
    fac_ref,
    spread_ref,
    summed_ref,
    dhid_ref,
    dtotal_ref,
    dlive_ref,
    dsum_ref,
    dz_ref,
    source_val,
    dst_val,
    back_ref,
    send_sem,
    recv_sem,
    send_sem2,
    recv_sem2,
):
    me = lax.axis_index(axis)
    width, atoms = atom_ref.shape
    bonds = bond_ref.shape[1]
    angles = first_ref.shape[1]
    groups = bonds // GROUP
    slots = list_ref.shape[1]
    bond_chunks = bonds // CHUNK
    angle_chunks = angles // CHUNK

    barrier = pltpu.get_barrier_semaphore()

    def greet(turn, carry):
        pl.semaphore_signal(
            barrier,
            inc=1,
            device_id={axis: lax.rem(me + turn, n)},
            device_id_type=pl.DeviceIdType.MESH,
        )
        return carry

    for k in (0, 3, 8, 9, 12, 13, 10, 11, 14, 15, 1, 2, 5, 4, 6, 7):
        copies[k].start()
    lax.fori_loop(1, n, greet, 0)

    def ready(*which):
        for k in which:
            copies[k].wait()

    def count_of(ref):
        hit = lax.broadcasted_iota(jnp.int32, ref.shape, 1) == me
        return jnp.sum(jnp.where(hit, ref[...].astype(F32), 0.0), axis=1, keepdims=True).astype(
            jnp.int32
        )

    def copy_to(source, target, sems, rsems, turn):
        there = lax.rem(me + turn, n)
        return pltpu.make_async_remote_copy(
            src_ref=source.at[there],
            dst_ref=target.at[me],
            send_sem=sems.at[turn],
            recv_sem=rsems.at[turn],
            device_id={axis: there},
            device_id_type=pl.DeviceIdType.MESH,
        )

    def start_all(source, target, sems, rsems):
        def one(turn, carry):
            copy_to(source, target, sems, rsems, turn).start()
            return carry

        lax.fori_loop(1, n, one, 0)

    def wait_all(source, target, sems, rsems):
        def one(turn, carry):
            copy_to(source, target, sems, rsems, turn).wait()
            return carry

        lax.fori_loop(1, n, one, 0)

    def at(chunk, base=0):
        return slice(base + chunk * CHUNK, base + (chunk + 1) * CHUNK)

    ready(0, 3, 8, 9)
    wo_t = flip(wo_ref[...])
    atom_back = dot(wo_t, acot_ref[...]).astype(BF16)
    own = jnp.concatenate([atom_ref[...], atom_back], 0)
    table_list = onehot(atoms, list_ref[...])
    listed = dot(own, table_list)
    send_ref[...] = jnp.transpose(listed).reshape(send_ref.shape).astype(BF16)
    own_atom = atom_ref[...]

    ready(12, 13)

    def angle_tables(turn, carry):
        cols = pl.ds(pl.multiple_of(turn * CHUNK, CHUNK), CHUNK)
        more = pl.ds(pl.multiple_of(angles + turn * CHUNK, CHUNK), CHUNK)
        fill_table(table_pair, first_ref[:, cols] & (GROUP - 1), cols)
        fill_table(table_pair, second_ref[:, cols] & (GROUP - 1), more)
        return carry

    lax.fori_loop(0, angle_chunks, angle_tables, 0)
    pl.semaphore_wait(barrier, n - 1)
    start_all(send_ref, recv_ref, send_sem, recv_sem)
    recv_ref[me] = send_ref[me]

    ready(10, 11, 14, 15)
    bond_count = count_of(bcount_ref)
    angle_count = count_of(acount_ref)

    def bond_tables(turn, carry):
        cols = pl.ds(pl.multiple_of(turn * CHUNK, CHUNK), CHUNK)
        live = lax.broadcasted_iota(jnp.int32, (1, CHUNK), 1) + turn * CHUNK < bond_count
        fill_table(table_source, src_ref[:, cols], cols)
        fill_table(table_dst, jnp.where(live, dst_ref[:, cols], -1), cols)
        return carry

    lax.fori_loop(0, bond_chunks, bond_tables, 0)

    ready(1, 2, 5)
    wa = wa_ref[...]
    wa_t = flip(wa[:, : 3 * width])
    for k in range(groups):
        stack_ref[k * width : (k + 1) * width, :] = bond_ref[:, k * GROUP : (k + 1) * GROUP]
    source = jnp.concatenate([src_ref[:, k * GROUP : (k + 1) * GROUP] for k in range(groups)], 0)
    stack_ref[groups * width :, :] = jnp.concatenate(
        [(source & (GROUP - 1)).astype(F32), (source // GROUP).astype(F32)], 0
    ).astype(BF16)

    def gather_first(chunk):
        group = first_ref[:, at(chunk)] // GROUP
        got = dot(stack_ref[...], table_pair[:, at(chunk)])
        zin_ref[width : 2 * width, at(chunk)] = pick_group(got, group, groups, width).astype(BF16)
        low = got[groups * width : groups * width + groups]
        high = got[groups * width + groups :]
        hit = lax.broadcasted_iota(jnp.int32, low.shape, 0) == group
        index = jnp.sum(jnp.where(hit, low + GROUP * high, 0.0), axis=0, keepdims=True)
        fill_table(table_source, index.astype(jnp.int32), at(chunk, bonds))

    def gather_second(chunk):
        group = second_ref[:, at(chunk)] // GROUP
        got = dot(stack_ref[: groups * width, :], table_pair[:, at(chunk, angles)])
        zin_ref[2 * width : 3 * width, at(chunk)] = pick_group(got, group, groups, width).astype(BF16)

    def own_angle(chunk):
        zin_ref[:width, at(chunk)] = dot(own_atom, table_source[:atoms, at(chunk, bonds)]).astype(BF16)

    def own_bond(chunk):
        bin_ref[:width, at(chunk)] = dot(own_atom, table_source[:atoms, at(chunk)]).astype(BF16)
        got = dot(own, table_dst[:atoms, at(chunk)]).astype(BF16)
        bin_ref[width : 2 * width, at(chunk)] = got[:width]
        up_ref[:, at(chunk)] = got[width:]

    for chunk in range(angle_chunks):
        gather_first(chunk)
    for chunk in range(angle_chunks):
        gather_second(chunk)
    for chunk in range(angle_chunks):
        own_angle(chunk)
    for chunk in range(bond_chunks):
        own_bond(chunk)

    ready(4, 6, 7)
    wb = wb_ref[...]
    wb_t = flip(wb)
    wm_t = wm_ref[...]
    wm = flip(wm_t)

    wait_all(send_ref, recv_ref, send_sem, recv_sem)
    received = jnp.transpose(recv_ref[...].astype(F32).reshape(slots, 2 * width)).astype(BF16)

    def first_group(chunk):
        place = lax.broadcasted_iota(jnp.int32, (1, CHUNK), 1) + chunk * CHUNK
        return jnp.where(place < angle_count, first_ref[:, at(chunk)] // GROUP, -1)

    def expand(value, group, cols):
        wide = wide_row(group)
        one = jnp.ones((16, CHUNK), BF16)
        zero = jnp.zeros((16, CHUNK), BF16)
        value = value.reshape(width // 16, 16, CHUNK)
        for k in range(groups):
            mask = jnp.where(wide == jnp.full((16, CHUNK), k, BF16), one, zero)
            spread_ref[k * width : (k + 1) * width, cols] = (value * mask[None]).reshape(width, CHUNK)

    def all_angle(chunk):
        got = dot(received[:width], table_source[atoms:, at(chunk, bonds)]).astype(BF16)
        zin_ref[:width, at(chunk)] = zin_ref[:width, at(chunk)] + got

    def all_bond(chunk):
        got = dot(received[:width], table_source[atoms:, at(chunk)]).astype(BF16)
        bin_ref[:width, at(chunk)] = bin_ref[:width, at(chunk)] + got
        got = dot(received, table_dst[atoms:, at(chunk)]).astype(BF16)
        bin_ref[width : 2 * width, at(chunk)] = bin_ref[width : 2 * width, at(chunk)] + got[:width]
        up_ref[:, at(chunk)] = up_ref[:, at(chunk)] + got[width:]

    def message(chunk):
        out, fac_a, fac_c = gate_parts(dot(wa, zin_ref[:, at(chunk)]))
        fac_ref[:width, at(chunk)] = fac_a.astype(BF16)
        fac_ref[width:, at(chunk)] = fac_c.astype(BF16)
        expand(out.astype(BF16), first_group(chunk), at(chunk))

    skewed(angle_chunks, all_angle, message)
    for chunk in range(bond_chunks):
        all_bond(chunk)
    summed = dot_nt(spread_ref[:, :angles], table_pair[:, :angles]).astype(BF16)
    for k in range(groups):
        summed_ref[:, k * GROUP : (k + 1) * GROUP] = summed[k * width : (k + 1) * width]


    def live_bond(chunk):
        return lax.broadcasted_iota(jnp.int32, (1, CHUNK), 1) + chunk * CHUNK < bond_count

    def update_bond(chunk):
        update = jnp.where(live_bond(chunk), dot(wb, summed_ref[:, at(chunk)]), 0.0)
        new_bond = (bond_ref[:, at(chunk)].astype(F32) + update).astype(BF16)
        new_bond_ref[:, at(chunk)] = new_bond
        bin_ref[2 * width :, at(chunk)] = new_bond

    def bond_message(chunk):
        out, fac_a, fac_c = gate_parts(dot(wm, bin_ref[:, at(chunk)]))
        up = up_ref[:, at(chunk)].astype(F32)
        dhid_ref[:width, at(chunk)] = (up * fac_a).astype(BF16)
        dhid_ref[width:, at(chunk)] = (up * fac_c).astype(BF16)
        dst_val[:width, at(chunk)] = out.astype(BF16)

    def bond_back(chunk):
        back = dot(wm_t, dhid_ref[:, at(chunk)])
        dtotal = bcot_ref[:, at(chunk)].astype(F32) + back[2 * width :]
        dtotal_ref[:, at(chunk)] = dtotal
        dlive_ref[:, at(chunk)] = jnp.where(live_bond(chunk), dtotal, 0.0).astype(BF16)
        source_val[:, at(chunk)] = back[:width].astype(BF16)
        dst_val[width:, at(chunk)] = back[width : 2 * width].astype(BF16)

    def summed_back(chunk):
        dsum = dot(wb_t, dlive_ref[:, at(chunk)]).astype(BF16)
        for k in range(CHUNK // GROUP):
            row = (chunk * (CHUNK // GROUP) + k) * width
            dsum_ref[row : row + width, :] = dsum[:, k * GROUP : (k + 1) * GROUP]

    skewed(bond_chunks, update_bond, bond_message, bond_back, summed_back)

    def angle_up(chunk):
        got = dot(dsum_ref[...], table_pair[:, at(chunk)])
        up = pick_group(got, first_group(chunk), groups, width).astype(BF16)
        dz_ref[:width, at(chunk)] = up * fac_ref[:width, at(chunk)]
        dz_ref[width:, at(chunk)] = up * fac_ref[width:, at(chunk)]

    def angle_back(chunk):
        back = dot(wa_t, dz_ref[:, at(chunk)]).astype(BF16)
        source_val[:, at(chunk, bonds)] = back[:width]
        back_ref[:, at(chunk)] = back[width:]

    skewed(angle_chunks, angle_up, angle_back)
    far_source = dot_nt(table_source[atoms:, :], source_val[...])
    far_dst = dot_nt(table_dst[atoms:, :], dst_val[...])
    far = jnp.concatenate([far_dst[:, :width], far_dst[:, width:] + far_source], 1)
    send2_ref[...] = far.reshape(send2_ref.shape).astype(BF16)

    start_all(send2_ref, recv2_ref, send_sem2, recv_sem2)
    recv2_ref[me] = send2_ref[me]

    def late(chunk):
        expand(back_ref[:width, at(chunk)], first_group(chunk), at(chunk))
        expand(back_ref[width:, at(chunk)], second_ref[:, at(chunk)] // GROUP, at(chunk, angles))

    near_source = dot_nt(table_source[:atoms, :], source_val[...])
    near_dst = dot_nt(table_dst[:atoms, :], dst_val[...])
    for chunk in range(angle_chunks):
        late(chunk)
    back = dot_nt(spread_ref[...], table_pair[...])
    for k in range(groups):
        cols = slice(k * GROUP, (k + 1) * GROUP)
        grad_bond_ref[:, cols] = (dtotal_ref[:, cols] + back[k * width : (k + 1) * width]).astype(BF16)

    wait_all(send2_ref, recv2_ref, send_sem2, recv_sem2)
    returned = dot(table_list, recv2_ref[...].reshape(slots, 2 * width))
    total = jnp.concatenate([near_dst[:, :width], near_dst[:, width:] + near_source], 1) + returned
    total = jnp.transpose(total)
    new_atom_ref[...] = (
        atom_ref[...].astype(F32) + dot(wo_ref[...], total[:width].astype(BF16))
    ).astype(BF16)
    grad_atom_ref[...] = (acot_ref[...].astype(F32) + total[width:]).astype(BF16)


def local(n, *args):
    (atom_feat, bond_feat, angle_feat) = args[:3]
    width, atoms = atom_feat.shape
    bonds = bond_feat.shape[1]
    angles = angle_feat.shape[1]
    slots = args[9].shape[1]
    groups = bonds // GROUP
    space_cols = atoms + slots
    args = list(args)
    for at in (10, 11, 13, 14):
        args[at] = args[at].reshape(1, -1)
    args[7] = args[7].T
    args = args[:12] + args[13:15] + [args[12].reshape(1, -1), args[15].reshape(1, -1)]
    vm = pl.BlockSpec(memory_space=pltpu.VMEM)
    anywhere = pl.BlockSpec(memory_space=pl.ANY)
    part = slots // n
    exchange = pltpu.VMEM((n, part, 2 * width), BF16)
    shapes = (atom_feat.shape, bond_feat.shape, atom_feat.shape, bond_feat.shape)
    held = pl.pallas_call(
        functools.partial(kernel, n, "dom"),
        out_shape=tuple(pltpu.VMEM(shape, BF16) for shape in shapes),
        in_specs=[anywhere] * INPUTS,
        out_specs=[vm] * 4,
        scratch_shapes=[
            pltpu.VMEM(arg.shape, arg.dtype) for k, arg in enumerate(args) if k != 2
        ]
        + [
            pltpu.SemaphoreType.DMA((INPUTS,)),
            pltpu.VMEM((4 * width, angles), BF16),
            exchange,
            exchange,
            exchange,
            exchange,
            pltpu.VMEM((GROUP, 2 * angles), BF16),
            pltpu.VMEM((space_cols, bonds + angles), BF16),
            pltpu.VMEM((space_cols, bonds), BF16),
            pltpu.VMEM((groups * width + 2 * groups, GROUP), BF16),
            pltpu.VMEM((3 * width, bonds), BF16),
            pltpu.VMEM((width, bonds), BF16),
            pltpu.VMEM((2 * width, angles), BF16),
            pltpu.VMEM((groups * width, 2 * angles), BF16),
            pltpu.VMEM((width, bonds), BF16),
            pltpu.VMEM((2 * width, bonds), BF16),
            pltpu.VMEM((width, bonds), F32),
            pltpu.VMEM((width, bonds), BF16),
            pltpu.VMEM((groups * width, GROUP), BF16),
            pltpu.VMEM((2 * width, angles), BF16),
            pltpu.VMEM((width, bonds + angles), BF16),
            pltpu.VMEM((2 * width, bonds), BF16),
            pltpu.VMEM((2 * width, angles), BF16),
            pltpu.SemaphoreType.DMA((n,)),
            pltpu.SemaphoreType.DMA((n,)),
            pltpu.SemaphoreType.DMA((n,)),
            pltpu.SemaphoreType.DMA((n,)),
        ],
        compiler_params=pltpu.CompilerParams(collective_id=0, has_side_effects=True),
    )(*args)
    return pl.pallas_call(
        write_out,
        out_shape=tuple(jax.ShapeDtypeStruct(shape, BF16) for shape in shapes),
        in_specs=[vm] * 4,
        out_specs=[pl.BlockSpec(memory_space=pl.ANY)] * 4,
        scratch_shapes=[pltpu.SemaphoreType.DMA((4,))],
    )(*(pltpu.with_memory_space_constraint(each, pltpu.VMEM) for each in held))


def write_out(*refs):
    sems = refs[8]
    copies = [pltpu.make_async_copy(refs[k], refs[4 + k], sems.at[k]) for k in range(4)]
    for copy in copies:
        copy.start()
    for copy in copies:
        copy.wait()


def solution(mesh):
    return jax.shard_map(
        functools.partial(local, mesh.shape["dom"]),
        mesh=mesh,
        in_specs=(
            P("member", "dom"),
            P("member", "dom"),
            P("member", "dom"),
            P("member", "dom"),
            P("member", "dom"),
            P("member", None),
            P("member", None),
            P("member", None),
            P("member", None),
            P("dom", None),
            P("dom"),
            P("dom"),
            P(),
            P("dom"),
            P("dom"),
            P(),
        ),
        out_specs=(P("member", "dom"), P("member", "dom"), P("member", "dom"), P("member", "dom")),
        check_vma=False,
    )
```

```python
import functools

import jax
import jax.numpy as jnp
from jax import lax
from jax.experimental import pallas as pl
from jax.experimental.pallas import tpu as pltpu
from jax.sharding import PartitionSpec as P

F32 = jnp.float32
BF16 = jnp.bfloat16
GROUP = 256
CHUNK = 512


def dot(a, b):
    return lax.dot_general(a, b, (((1,), (0,)), ((), ())), preferred_element_type=F32)


def dot_nt(a, b):
    return lax.dot_general(a, b, (((1,), (1,)), ((), ())), preferred_element_type=F32)


def flip(a):
    return jnp.transpose(a.astype(F32)).astype(BF16)


def onehot(rows, index):
    grid = lax.broadcasted_iota(jnp.int32, (rows, index.shape[1]), 0)
    return jnp.where(grid == index, 1.0, 0.0).astype(BF16)


def wide_row(index, rows=16):
    return jnp.broadcast_to(index, (rows, index.shape[1])).astype(F32).astype(BF16)


def fill_table(table, index, cols):
    rows = table.shape[0]
    step = lax.broadcasted_iota(jnp.int32, (16, CHUNK), 0).astype(F32).astype(BF16)
    one = jnp.ones((16, CHUNK), BF16)
    zero = jnp.zeros((16, CHUNK), BF16)
    for base in range(0, rows, GROUP):
        wide = wide_row(index - base)
        for at in range(0, min(GROUP, rows - base), 16):
            table[base + at : base + at + 16, cols] = jnp.where(wide == step + at, one, zero)


def gate_parts(value):
    half = value.shape[0] // 2
    first = value[:half]
    sig_a = 0.5 * jnp.tanh(0.5 * first) + 0.5
    sig_c = 0.5 * jnp.tanh(0.5 * value[half:]) + 0.5
    prod = first * sig_a
    out = prod * sig_c
    return out, sig_c * (sig_a + prod * (1.0 - sig_a)), out * (1.0 - sig_c)


def pick_group(stacked, group, groups, width):
    acc = jnp.zeros((width, stacked.shape[1]), F32)
    group = jnp.broadcast_to(group, acc.shape)
    for k in range(groups):
        acc = jnp.where(group == k, stacked[k * width : (k + 1) * width], acc)
    return acc


def skewed(count, *stages):
    for turn in range(count + len(stages) - 1):
        for late in reversed(range(len(stages))):
            if 0 <= turn - late < count:
                stages[late](turn - late)


INPUTS = 16
PER_G = 2
PER_O = 2
PER_M = 2
PER_B = 4
PER_C = 2
PER_L = 2


def kernel(n, axis, *refs):
    sources = refs[:INPUTS]
    outs = refs[INPUTS : INPUTS + 4]
    staged = list(refs[INPUTS + 4 : 2 * INPUTS + 3])
    in_sem, zin_ref = refs[2 * INPUTS + 3 : 2 * INPUTS + 5]
    width = sources[0].shape[0]
    staged.insert(2, zin_ref.at[3 * width : 4 * width, :])
    copies = [
        pltpu.make_async_copy(sources[k], staged[k], in_sem.at[k]) for k in range(INPUTS)
    ]
    body(n, axis, copies, *staged, *outs, zin_ref, *refs[2 * INPUTS + 5 :])


def body(
    n,
    axis,
    copies,
    atom_ref,
    bond_ref,
    angle_ref,
    acot_ref,
    bcot_ref,
    wa_ref,
    wb_ref,
    wm_ref,
    wo_ref,
    list_ref,
    src_ref,
    dst_ref,
    first_ref,
    second_ref,
    bcount_ref,
    acount_ref,
    new_atom_ref,
    new_bond_ref,
    grad_atom_ref,
    grad_bond_ref,
    zin_ref,
    send_ref,
    recv_ref,
    send2_ref,
    recv2_ref,
    table_pair,
    table_source,
    table_dst,
    stack_ref,
    bin_ref,
    up_ref,
    fac_ref,
    spread_ref,
    summed_ref,
    dhid_ref,
    dtotal_ref,
    dlive_ref,
    dsum_ref,
    dz_ref,
    source_val,
    dst_val,
    back_ref,
    near_ref,
    send_sem,
    recv_sem,
    send_sem2,
    recv_sem2,
):
    me = lax.axis_index(axis)
    width, atoms = atom_ref.shape
    bonds = bond_ref.shape[1]
    angles = first_ref.shape[1]
    groups = bonds // GROUP
    slots = list_ref.shape[1]
    bond_chunks = bonds // CHUNK
    angle_chunks = angles // CHUNK

    barrier = pltpu.get_barrier_semaphore()

    def greet(turn, carry):
        pl.semaphore_signal(
            barrier,
            inc=1,
            device_id={axis: lax.rem(me + turn, n)},
            device_id_type=pl.DeviceIdType.MESH,
        )
        return carry

    for k in (0, 3, 8, 9, 12, 13, 10, 11, 14, 15, 1, 2, 5, 4, 6, 7):
        copies[k].start()
    lax.fori_loop(1, n, greet, 0)

    def ready(*which):
        for k in which:
            copies[k].wait()

    def count_of(ref):
        hit = lax.broadcasted_iota(jnp.int32, ref.shape, 1) == me
        return jnp.sum(jnp.where(hit, ref[...].astype(F32), 0.0), axis=1, keepdims=True).astype(
            jnp.int32
        )

    def copy_to(source, target, sems, rsems, turn):
        there = lax.rem(me + turn, n)
        return pltpu.make_async_remote_copy(
            src_ref=source.at[there],
            dst_ref=target.at[me],
            send_sem=sems,
            recv_sem=rsems,
            device_id={axis: there},
            device_id_type=pl.DeviceIdType.MESH,
        )

    def start_all(source, target, sems, rsems):
        def one(turn, carry):
            copy_to(source, target, sems, rsems, turn).start()
            return carry

        lax.fori_loop(1, n, one, 0)

    def wait_all(source, target, sems, rsems):
        pltpu.make_async_remote_copy(
            src_ref=source.at[pl.ds(0, n - 1)],
            dst_ref=target.at[pl.ds(0, n - 1)],
            send_sem=sems,
            recv_sem=rsems,
            device_id={axis: lax.rem(me + 1, n)},
            device_id_type=pl.DeviceIdType.MESH,
        ).wait()

    def at(chunk, base=0):
        return pl.ds(pl.multiple_of(base + chunk * CHUNK, CHUNK), CHUNK)

    once = 1 + jnp.minimum(me, 0)

    def staged(count, per, *stages):
        def turn_of(turn, carry):
            skewed(per, *(lambda k, stage=stage: stage(turn * per + k) for stage in stages))
            return carry

        lax.fori_loop(0, count // per if count > per else once, turn_of, 0)

    def region(work):
        def turn_of(turn, carry):
            work()
            return carry

        lax.fori_loop(0, once, turn_of, 0)

    def scatter(value, table, low, high):
        middle = (low + high) // 2
        return dot_nt(value[:, low:middle], table[:, low:middle]) + dot_nt(
            value[:, middle:high], table[:, middle:high]
        )

    ready(0, 3, 8, 9)
    wo_t = flip(wo_ref[...])
    atom_back = dot(wo_t, acot_ref[...]).astype(BF16)
    own = jnp.concatenate([atom_ref[...], atom_back], 0)
    table_list = onehot(atoms, list_ref[...])
    listed = dot(own, table_list)
    send_ref[...] = jnp.transpose(listed).reshape(send_ref.shape).astype(BF16)
    own_atom = atom_ref[...]

    ready(12, 13)

    def angle_tables(turn, carry):
        cols = pl.ds(pl.multiple_of(turn * CHUNK, CHUNK), CHUNK)
        more = pl.ds(pl.multiple_of(angles + turn * CHUNK, CHUNK), CHUNK)
        fill_table(table_pair, first_ref[:, cols] & (GROUP - 1), cols)
        fill_table(table_pair, second_ref[:, cols] & (GROUP - 1), more)
        return carry

    lax.fori_loop(0, angle_chunks, angle_tables, 0)
    pl.semaphore_wait(barrier, n - 1)
    start_all(send_ref, recv_ref, send_sem, recv_sem)
    recv_ref[me] = send_ref[me]

    ready(10, 11, 14, 15)
    bond_count = count_of(bcount_ref)
    angle_count = count_of(acount_ref)

    def bond_tables(turn, carry):
        cols = pl.ds(pl.multiple_of(turn * CHUNK, CHUNK), CHUNK)
        live = lax.broadcasted_iota(jnp.int32, (1, CHUNK), 1) + turn * CHUNK < bond_count
        fill_table(table_source, src_ref[:, cols], cols)
        fill_table(table_dst, jnp.where(live, dst_ref[:, cols], -1), cols)
        return carry

    lax.fori_loop(0, bond_chunks, bond_tables, 0)

    ready(1, 2, 5)
    wa = wa_ref[...]
    wa_t = flip(wa[:, : 3 * width])
    for k in range(groups):
        stack_ref[k * width : (k + 1) * width, :] = bond_ref[:, k * GROUP : (k + 1) * GROUP]
    source = jnp.concatenate([src_ref[:, k * GROUP : (k + 1) * GROUP] for k in range(groups)], 0)
    stack_ref[groups * width :, :] = jnp.concatenate(
        [(source & (GROUP - 1)).astype(F32), (source // GROUP).astype(F32)], 0
    ).astype(BF16)

    def gather_first(chunk):
        group = first_ref[:, at(chunk)] // GROUP
        got = dot(stack_ref[...], table_pair[:, at(chunk)])
        zin_ref[width : 2 * width, at(chunk)] = pick_group(got, group, groups, width).astype(BF16)
        low = got[groups * width : groups * width + groups]
        high = got[groups * width + groups :]
        hit = lax.broadcasted_iota(jnp.int32, low.shape, 0) == group
        index = jnp.sum(jnp.where(hit, low + GROUP * high, 0.0), axis=0, keepdims=True)
        fill_table(table_source, index.astype(jnp.int32), at(chunk, bonds))

    def gather_second(chunk):
        group = second_ref[:, at(chunk)] // GROUP
        got = dot(stack_ref[: groups * width, :], table_pair[:, at(chunk, angles)])
        zin_ref[2 * width : 3 * width, at(chunk)] = pick_group(got, group, groups, width).astype(BF16)

    def own_angle(chunk):
        zin_ref[:width, at(chunk)] = dot(own_atom, table_source[:atoms, at(chunk, bonds)]).astype(BF16)

    def own_bond(chunk):
        bin_ref[:width, at(chunk)] = dot(own_atom, table_source[:atoms, at(chunk)]).astype(BF16)
        got = dot(own, table_dst[:atoms, at(chunk)]).astype(BF16)
        bin_ref[width : 2 * width, at(chunk)] = got[:width]
        up_ref[:, at(chunk)] = got[width:]

    staged(angle_chunks, PER_G, gather_first, gather_second)
    staged(angle_chunks, PER_O, own_angle, own_bond)

    ready(4, 6, 7)
    wb = wb_ref[...]
    wb_t = flip(wb)
    wm_t = wm_ref[...]
    wm = flip(wm_t)

    wait_all(send_ref, recv_ref, send_sem, recv_sem)
    received = jnp.transpose(recv_ref[...].astype(F32).reshape(slots, 2 * width)).astype(BF16)

    def first_group(chunk):
        place = lax.broadcasted_iota(jnp.int32, (1, CHUNK), 1) + chunk * CHUNK
        return jnp.where(place < angle_count, first_ref[:, at(chunk)] // GROUP, -1)

    def expand(value, group, cols):
        wide = wide_row(group)
        one = jnp.ones((16, CHUNK), BF16)
        zero = jnp.zeros((16, CHUNK), BF16)
        value = value.reshape(width // 16, 16, CHUNK)
        for k in range(groups):
            mask = jnp.where(wide == jnp.full((16, CHUNK), k, BF16), one, zero)
            spread_ref[k * width : (k + 1) * width, cols] = (value * mask[None]).reshape(width, CHUNK)

    def all_angle(chunk):
        got = dot(received[:width], table_source[atoms:, at(chunk, bonds)]).astype(BF16)
        zin_ref[:width, at(chunk)] = zin_ref[:width, at(chunk)] + got

    def all_bond(chunk):
        got = dot(received[:width], table_source[atoms:, at(chunk)]).astype(BF16)
        bin_ref[:width, at(chunk)] = bin_ref[:width, at(chunk)] + got
        got = dot(received, table_dst[atoms:, at(chunk)]).astype(BF16)
        bin_ref[width : 2 * width, at(chunk)] = bin_ref[width : 2 * width, at(chunk)] + got[:width]
        up_ref[:, at(chunk)] = up_ref[:, at(chunk)] + got[width:]

    def message(chunk):
        out, fac_a, fac_c = gate_parts(dot(wa, zin_ref[:, at(chunk)]))
        fac_ref[:width, at(chunk)] = fac_a.astype(BF16)
        fac_ref[width:, at(chunk)] = fac_c.astype(BF16)
        expand(out.astype(BF16), first_group(chunk), at(chunk))

    staged(angle_chunks, PER_M, all_angle, message)
    staged(bond_chunks, PER_O, all_bond)

    def sum_messages():
        summed = scatter(spread_ref, table_pair, 0, angles).astype(BF16)
        for k in range(groups):
            summed_ref[:, k * GROUP : (k + 1) * GROUP] = summed[k * width : (k + 1) * width]

    region(sum_messages)


    def live_bond(chunk):
        return lax.broadcasted_iota(jnp.int32, (1, CHUNK), 1) + chunk * CHUNK < bond_count

    def update_bond(chunk):
        update = jnp.where(live_bond(chunk), dot(wb, summed_ref[:, at(chunk)]), 0.0)
        new_bond = (bond_ref[:, at(chunk)].astype(F32) + update).astype(BF16)
        new_bond_ref[:, at(chunk)] = new_bond
        bin_ref[2 * width :, at(chunk)] = new_bond

    def bond_message(chunk):
        out, fac_a, fac_c = gate_parts(dot(wm, bin_ref[:, at(chunk)]))
        up = up_ref[:, at(chunk)].astype(F32)
        dhid_ref[:width, at(chunk)] = (up * fac_a).astype(BF16)
        dhid_ref[width:, at(chunk)] = (up * fac_c).astype(BF16)
        dst_val[:width, at(chunk)] = out.astype(BF16)

    def bond_back(chunk):
        back = dot(wm_t, dhid_ref[:, at(chunk)])
        dtotal = bcot_ref[:, at(chunk)].astype(F32) + back[2 * width :]
        dtotal_ref[:, at(chunk)] = dtotal
        dlive_ref[:, at(chunk)] = jnp.where(live_bond(chunk), dtotal, 0.0).astype(BF16)
        source_val[:, at(chunk)] = back[:width].astype(BF16)
        dst_val[width:, at(chunk)] = back[width : 2 * width].astype(BF16)

    def summed_back(chunk):
        dsum = dot(wb_t, dlive_ref[:, at(chunk)]).astype(BF16)
        for k in range(CHUNK // GROUP):
            row = pl.multiple_of((chunk * (CHUNK // GROUP) + k) * width, width)
            dsum_ref[pl.ds(row, width), :] = dsum[:, k * GROUP : (k + 1) * GROUP]

    staged(bond_chunks, PER_B, update_bond, bond_message, bond_back, summed_back)

    def angle_up(chunk):
        got = dot(dsum_ref[...], table_pair[:, at(chunk)])
        up = pick_group(got, first_group(chunk), groups, width).astype(BF16)
        dz_ref[:width, at(chunk)] = up * fac_ref[:width, at(chunk)]
        dz_ref[width:, at(chunk)] = up * fac_ref[width:, at(chunk)]

    def angle_back(chunk):
        back = dot(wa_t, dz_ref[:, at(chunk)]).astype(BF16)
        source_val[:, at(chunk, bonds)] = back[:width]
        back_ref[:, at(chunk)] = back[width:]

    staged(angle_chunks, PER_C, angle_up, angle_back)

    def pooled_rows(rows):
        parts = [
            dot_nt(table_source[rows, :bonds], source_val[:, :bonds]),
            dot_nt(table_source[rows, bonds:], source_val[:, bonds:]),
        ]
        half = bonds // 2
        both = dot_nt(table_dst[rows, :half], dst_val[:, :half]) + dot_nt(
            table_dst[rows, half:], dst_val[:, half:]
        )
        return jnp.concatenate([both[:, :width], both[:, width:] + parts[0] + parts[1]], 1)

    def far_rows():
        far = pooled_rows(slice(atoms, atoms + slots))
        send2_ref[...] = far.reshape(send2_ref.shape).astype(BF16)

    region(far_rows)

    start_all(send2_ref, recv2_ref, send_sem2, recv_sem2)
    recv2_ref[me] = send2_ref[me]

    def late(chunk):
        expand(back_ref[:width, at(chunk)], first_group(chunk), at(chunk))
        expand(back_ref[width:, at(chunk)], second_ref[:, at(chunk)] // GROUP, at(chunk, angles))

    def near_rows():
        near_ref[...] = pooled_rows(slice(0, atoms))

    region(near_rows)
    staged(angle_chunks, PER_L, late)

    def bond_grads():
        back = scatter(spread_ref, table_pair, 0, 2 * angles)
        for k in range(groups):
            cols = slice(k * GROUP, (k + 1) * GROUP)
            grad_bond_ref[:, cols] = (
                dtotal_ref[:, cols] + back[k * width : (k + 1) * width]
            ).astype(BF16)

    region(bond_grads)

    wait_all(send2_ref, recv2_ref, send_sem2, recv_sem2)
    returned = dot(table_list, recv2_ref[...].reshape(slots, 2 * width))
    total = jnp.transpose(near_ref[...] + returned)
    new_atom_ref[...] = (
        atom_ref[...].astype(F32) + dot(wo_ref[...], total[:width].astype(BF16))
    ).astype(BF16)
    grad_atom_ref[...] = (acot_ref[...].astype(F32) + total[width:]).astype(BF16)


def local(n, *args):
    (atom_feat, bond_feat, angle_feat) = args[:3]
    width, atoms = atom_feat.shape
    bonds = bond_feat.shape[1]
    angles = angle_feat.shape[1]
    slots = args[9].shape[1]
    groups = bonds // GROUP
    space_cols = atoms + slots
    args = list(args)
    for at in (10, 11, 13, 14):
        args[at] = args[at].reshape(1, -1)
    args[7] = args[7].T
    args = args[:12] + args[13:15] + [args[12].reshape(1, -1), args[15].reshape(1, -1)]
    vm = pl.BlockSpec(memory_space=pltpu.VMEM)
    anywhere = pl.BlockSpec(memory_space=pl.ANY)
    part = slots // n
    exchange = pltpu.VMEM((n, part, 2 * width), BF16)
    shapes = (atom_feat.shape, bond_feat.shape, atom_feat.shape, bond_feat.shape)
    held = pl.pallas_call(
        functools.partial(kernel, n, "dom"),
        out_shape=tuple(pltpu.VMEM(shape, BF16) for shape in shapes),
        in_specs=[anywhere] * INPUTS,
        out_specs=[vm] * 4,
        scratch_shapes=[
            pltpu.VMEM(arg.shape, arg.dtype) for k, arg in enumerate(args) if k != 2
        ]
        + [
            pltpu.SemaphoreType.DMA((INPUTS,)),
            pltpu.VMEM((4 * width, angles), BF16),
            exchange,
            exchange,
            exchange,
            exchange,
            pltpu.VMEM((GROUP, 2 * angles), BF16),
            pltpu.VMEM((space_cols, bonds + angles), BF16),
            pltpu.VMEM((space_cols, bonds), BF16),
            pltpu.VMEM((groups * width + 2 * groups, GROUP), BF16),
            pltpu.VMEM((3 * width, bonds), BF16),
            pltpu.VMEM((width, bonds), BF16),
            pltpu.VMEM((2 * width, angles), BF16),
            pltpu.VMEM((groups * width, 2 * angles), BF16),
            pltpu.VMEM((width, bonds), BF16),
            pltpu.VMEM((2 * width, bonds), BF16),
            pltpu.VMEM((width, bonds), F32),
            pltpu.VMEM((width, bonds), BF16),
            pltpu.VMEM((groups * width, GROUP), BF16),
            pltpu.VMEM((2 * width, angles), BF16),
            pltpu.VMEM((width, bonds + angles), BF16),
            pltpu.VMEM((2 * width, bonds), BF16),
            pltpu.VMEM((2 * width, angles), BF16),
            pltpu.VMEM((atoms, 2 * width), F32),
            pltpu.SemaphoreType.DMA,
            pltpu.SemaphoreType.DMA,
            pltpu.SemaphoreType.DMA,
            pltpu.SemaphoreType.DMA,
        ],
        compiler_params=pltpu.CompilerParams(collective_id=0, has_side_effects=True),
    )(*args)
    return pl.pallas_call(
        write_out,
        out_shape=tuple(jax.ShapeDtypeStruct(shape, BF16) for shape in shapes),
        in_specs=[vm] * 4,
        out_specs=[pl.BlockSpec(memory_space=pl.ANY)] * 4,
        scratch_shapes=[pltpu.SemaphoreType.DMA((4,))],
    )(*(pltpu.with_memory_space_constraint(each, pltpu.VMEM) for each in held))


def write_out(*refs):
    sems = refs[8]
    copies = [pltpu.make_async_copy(refs[k], refs[4 + k], sems.at[k]) for k in range(4)]
    for copy in copies:
        copy.start()
    for copy in copies:
        copy.wait()


def solution(mesh):
    return jax.shard_map(
        functools.partial(local, mesh.shape["dom"]),
        mesh=mesh,
        in_specs=(
            P("member", "dom"),
            P("member", "dom"),
            P("member", "dom"),
            P("member", "dom"),
            P("member", "dom"),
            P("member", None),
            P("member", None),
            P("member", None),
            P("member", None),
            P("dom", None),
            P("dom"),
            P("dom"),
            P(),
            P("dom"),
            P("dom"),
            P(),
        ),
        out_specs=(P("member", "dom"), P("member", "dom"), P("member", "dom"), P("member", "dom")),
        check_vma=False,
    )
```

```python
import functools

import jax
import jax.numpy as jnp
from jax import lax
from jax.experimental import pallas as pl
from jax.experimental.pallas import tpu as pltpu
from jax.sharding import PartitionSpec as P

F32 = jnp.float32
BF16 = jnp.bfloat16
GROUP = 256
CHUNK = 512


def dot(a, b):
    return lax.dot_general(a, b, (((1,), (0,)), ((), ())), preferred_element_type=F32)


def dot_nt(a, b):
    return lax.dot_general(a, b, (((1,), (1,)), ((), ())), preferred_element_type=F32)


def flip(a):
    return jnp.transpose(a.astype(F32)).astype(BF16)


def onehot(rows, index):
    grid = lax.broadcasted_iota(jnp.int32, (rows, index.shape[1]), 0)
    return jnp.where(grid == index, 1.0, 0.0).astype(BF16)


def wide_row(index, rows=16):
    return jnp.broadcast_to(index, (rows, index.shape[1])).astype(F32).astype(BF16)


def fill_table(table, index, cols):
    rows = table.shape[0]
    step = lax.broadcasted_iota(jnp.int32, (16, CHUNK), 0).astype(F32).astype(BF16)
    one = jnp.ones((16, CHUNK), BF16)
    zero = jnp.zeros((16, CHUNK), BF16)
    for base in range(0, rows, GROUP):
        wide = wide_row(index - base)
        for at in range(0, min(GROUP, rows - base), 16):
            table[base + at : base + at + 16, cols] = jnp.where(wide == step + at, one, zero)


def gate_parts(halved):
    half = halved.shape[0] // 2
    first = halved[:half]
    wide = 1.0 + jnp.tanh(first)
    sig_a = 0.5 * wide
    sig_c = 0.5 * jnp.tanh(halved[half:]) + 0.5
    prod = first * wide
    out = prod * sig_c
    return out, sig_c * (sig_a + prod * (1.0 - sig_a)), out * (1.0 - sig_c)


def pick_group(stacked, group, groups, width):
    acc = jnp.zeros((width, stacked.shape[1]), F32)
    group = jnp.broadcast_to(group, acc.shape)
    for k in range(groups):
        acc = jnp.where(group == k, stacked[k * width : (k + 1) * width], acc)
    return acc


def skewed(count, *stages):
    for turn in range(count + len(stages) - 1):
        for late in reversed(range(len(stages))):
            if 0 <= turn - late < count:
                stages[late](turn - late)


INPUTS = 16
OUTPUTS = 6
PER_G = 2
PER_O = 2
PER_M = 2
PER_B = 4
PER_L = 2


def kernel(n, axis, *refs):
    sources = refs[:INPUTS]
    outs = refs[INPUTS : INPUTS + OUTPUTS]
    refs = refs[INPUTS + OUTPUTS :]
    staged = list(refs[: INPUTS - 1])
    in_sem, zin_ref = refs[INPUTS - 1 : INPUTS + 1]
    width = sources[0].shape[0]
    staged.insert(2, zin_ref.at[3 * width : 4 * width, :])
    copies = [
        pltpu.make_async_copy(sources[k], staged[k], in_sem.at[k]) for k in range(INPUTS)
    ]
    body(n, axis, copies, *staged, *outs, zin_ref, *refs[INPUTS + 1 :])


def body(
    n,
    axis,
    copies,
    atom_ref,
    bond_ref,
    angle_ref,
    acot_ref,
    bcot_ref,
    wa_ref,
    wb_ref,
    wm_ref,
    wo_ref,
    list_ref,
    src_ref,
    dst_ref,
    first_ref,
    second_ref,
    bcount_ref,
    acount_ref,
    total_ref,
    new_bond_ref,
    grad_bond_ref,
    kept_atom_ref,
    kept_cot_ref,
    kept_weight_ref,
    zin_ref,
    send_ref,
    recv_ref,
    send2_ref,
    recv2_ref,
    table_pair,
    table_source,
    table_dst,
    stack_ref,
    bin_ref,
    up_ref,
    fac_ref,
    spread_ref,
    summed_ref,
    dhid_ref,
    dtotal_ref,
    dlive_ref,
    dsum_ref,
    dz_ref,
    source_val,
    dst_val,
    back_ref,
    near_ref,
    z_ref,
    send_sem,
    recv_sem,
    send_sem2,
    recv_sem2,
):
    me = lax.axis_index(axis)
    width, atoms = atom_ref.shape
    bonds = bond_ref.shape[1]
    angles = first_ref.shape[1]
    groups = bonds // GROUP
    slots = list_ref.shape[1]
    bond_chunks = bonds // CHUNK
    angle_chunks = angles // CHUNK

    barrier = pltpu.get_barrier_semaphore()

    def greet(turn, carry):
        pl.semaphore_signal(
            barrier,
            inc=1,
            device_id={axis: lax.rem(me + turn, n)},
            device_id_type=pl.DeviceIdType.MESH,
        )
        return carry

    for k in (0, 3, 8, 9, 12, 13, 10, 11, 14, 15, 1, 2, 5, 4, 6, 7):
        copies[k].start()
    lax.fori_loop(1, n, greet, 0)

    def ready(*which):
        for k in which:
            copies[k].wait()

    def count_of(ref):
        hit = lax.broadcasted_iota(jnp.int32, ref.shape, 1) == me
        return jnp.sum(jnp.where(hit, ref[...].astype(F32), 0.0), axis=1, keepdims=True).astype(
            jnp.int32
        )

    def copy_to(source, target, sems, rsems, turn):
        there = lax.rem(me + turn, n)
        return pltpu.make_async_remote_copy(
            src_ref=source.at[there],
            dst_ref=target.at[me],
            send_sem=sems,
            recv_sem=rsems,
            device_id={axis: there},
            device_id_type=pl.DeviceIdType.MESH,
        )

    def start_all(source, target, sems, rsems):
        def one(turn, carry):
            copy_to(source, target, sems, rsems, turn).start()
            return carry

        lax.fori_loop(1, n, one, 0)

    def wait_all(source, target, sems, rsems):
        pltpu.make_async_remote_copy(
            src_ref=source.at[pl.ds(0, n - 1)],
            dst_ref=target.at[pl.ds(0, n - 1)],
            send_sem=sems,
            recv_sem=rsems,
            device_id={axis: lax.rem(me + 1, n)},
            device_id_type=pl.DeviceIdType.MESH,
        ).wait()

    def at(chunk, base=0):
        return pl.ds(pl.multiple_of(base + chunk * CHUNK, CHUNK), CHUNK)

    once = 1 + jnp.minimum(me, 0)

    def staged(count, per, *stages):
        def turn_of(turn, carry):
            skewed(per, *(lambda k, stage=stage: stage(turn * per + k) for stage in stages))
            return carry

        lax.fori_loop(0, count // per if count > per else once, turn_of, 0)

    def region(work):
        def turn_of(turn, carry):
            work()
            return carry

        lax.fori_loop(0, once, turn_of, 0)

    def scatter(value, table, low, high):
        middle = (low + high) // 2
        return dot_nt(value[:, low:middle], table[:, low:middle]) + dot_nt(
            value[:, middle:high], table[:, middle:high]
        )

    ready(0, 3, 8, 9)
    wo_t = flip(wo_ref[...])
    atom_back = dot(wo_t, acot_ref[...]).astype(BF16)
    own = jnp.concatenate([atom_ref[...], atom_back], 0)
    table_list = onehot(atoms, list_ref[...])
    listed = dot(own, table_list)
    send_ref[...] = jnp.transpose(listed).reshape(send_ref.shape).astype(BF16)
    own_atom = atom_ref[...]

    ready(12, 13)

    def angle_tables(turn, carry):
        cols = pl.ds(pl.multiple_of(turn * CHUNK, CHUNK), CHUNK)
        more = pl.ds(pl.multiple_of(angles + turn * CHUNK, CHUNK), CHUNK)
        fill_table(table_pair, first_ref[:, cols] & (GROUP - 1), cols)
        fill_table(table_pair, second_ref[:, cols] & (GROUP - 1), more)
        return carry

    lax.fori_loop(0, angle_chunks, angle_tables, 0)
    ready(10, 11, 14, 15)
    bond_count = count_of(bcount_ref)
    angle_count = count_of(acount_ref)

    def bond_tables(turn, carry):
        cols = pl.ds(pl.multiple_of(turn * CHUNK, CHUNK), CHUNK)
        live = lax.broadcasted_iota(jnp.int32, (1, CHUNK), 1) + turn * CHUNK < bond_count
        fill_table(table_source, src_ref[:, cols], cols)
        fill_table(table_dst, jnp.where(live, dst_ref[:, cols], -1), cols)
        return carry

    lax.fori_loop(0, bond_chunks, bond_tables, 0)

    pl.semaphore_wait(barrier, n - 1)
    start_all(send_ref, recv_ref, send_sem, recv_sem)
    recv_ref[me] = send_ref[me]

    ready(1, 2, 5)
    wa = wa_ref[...]
    wa_t = flip(wa[:, : 3 * width])
    for k in range(groups):
        stack_ref[k * width : (k + 1) * width, :] = bond_ref[:, k * GROUP : (k + 1) * GROUP]
    source = jnp.concatenate([src_ref[:, k * GROUP : (k + 1) * GROUP] for k in range(groups)], 0)
    stack_ref[groups * width :, :] = jnp.concatenate(
        [(source & (GROUP - 1)).astype(F32), (source // GROUP).astype(F32)], 0
    ).astype(BF16)

    def gather_first(chunk):
        group = first_ref[:, at(chunk)] // GROUP
        got = dot(stack_ref[...], table_pair[:, at(chunk)])
        zin_ref[width : 2 * width, at(chunk)] = pick_group(got, group, groups, width).astype(BF16)
        low = got[groups * width : groups * width + groups]
        high = got[groups * width + groups :]
        hit = lax.broadcasted_iota(jnp.int32, low.shape, 0) == group
        index = jnp.sum(jnp.where(hit, low + GROUP * high, 0.0), axis=0, keepdims=True)
        fill_table(table_source, index.astype(jnp.int32), at(chunk, bonds))

    def gather_second(chunk):
        group = second_ref[:, at(chunk)] // GROUP
        got = dot(stack_ref[: groups * width, :], table_pair[:, at(chunk, angles)])
        zin_ref[2 * width : 3 * width, at(chunk)] = pick_group(got, group, groups, width).astype(BF16)

    wa_half = wa * 0.5

    def own_angle(chunk):
        zin_ref[:width, at(chunk)] = dot(own_atom, table_source[:atoms, at(chunk, bonds)]).astype(BF16)

    def own_sum(chunk):
        z_ref[:, at(chunk)] = dot(wa_half, zin_ref[:, at(chunk)])

    def own_bond(chunk):
        bin_ref[:width, at(chunk)] = dot(own_atom, table_source[:atoms, at(chunk)]).astype(BF16)
        got = dot(own, table_dst[:atoms, at(chunk)]).astype(BF16)
        bin_ref[width : 2 * width, at(chunk)] = got[:width]
        up_ref[:, at(chunk)] = got[width:]

    staged(angle_chunks, PER_G, gather_first, gather_second)
    staged(angle_chunks, PER_O, own_angle, own_bond, own_sum)

    ready(4, 6, 7)
    wb = wb_ref[...]
    wb_t = flip(wb)
    wm_t = wm_ref[...]
    wm_half = flip(wm_t) * 0.5

    wait_all(send_ref, recv_ref, send_sem, recv_sem)
    received = jnp.transpose(recv_ref[...].astype(F32).reshape(slots, 2 * width)).astype(BF16)

    def first_group(chunk):
        place = lax.broadcasted_iota(jnp.int32, (1, CHUNK), 1) + chunk * CHUNK
        return jnp.where(place < angle_count, first_ref[:, at(chunk)] // GROUP, -1)

    def expand(value, group, cols):
        wide = wide_row(group)
        one = jnp.ones((16, CHUNK), BF16)
        zero = jnp.zeros((16, CHUNK), BF16)
        value = value.reshape(width // 16, 16, CHUNK)
        for k in range(groups):
            mask = jnp.where(wide == jnp.full((16, CHUNK), k, BF16), one, zero)
            spread_ref[k * width : (k + 1) * width, cols] = (value * mask[None]).reshape(width, CHUNK)

    def all_bond(chunk):
        got = dot(received[:width], table_source[atoms:, at(chunk)]).astype(BF16)
        bin_ref[:width, at(chunk)] = bin_ref[:width, at(chunk)] + got
        got = dot(received, table_dst[atoms:, at(chunk)]).astype(BF16)
        bin_ref[width : 2 * width, at(chunk)] = bin_ref[width : 2 * width, at(chunk)] + got[:width]
        up_ref[:, at(chunk)] = up_ref[:, at(chunk)] + got[width:]

    reach = dot(wa_half[:, :width], received[:width]).astype(BF16)

    def message(chunk):
        z_half = z_ref[:, at(chunk)] + dot(reach, table_source[atoms:, at(chunk, bonds)])
        out, fac_a, fac_c = gate_parts(z_half)
        fac_ref[:width, at(chunk)] = fac_a.astype(BF16)
        fac_ref[width:, at(chunk)] = fac_c.astype(BF16)
        expand(out.astype(BF16), first_group(chunk), at(chunk))

    staged(angle_chunks, PER_M, message, all_bond)

    def sum_messages():
        summed = scatter(spread_ref, table_pair, 0, angles).astype(BF16)
        for k in range(groups):
            summed_ref[:, k * GROUP : (k + 1) * GROUP] = summed[k * width : (k + 1) * width]

    region(sum_messages)


    def live_bond(chunk):
        return lax.broadcasted_iota(jnp.int32, (1, CHUNK), 1) + chunk * CHUNK < bond_count

    def update_bond(chunk):
        update = jnp.where(live_bond(chunk), dot(wb, summed_ref[:, at(chunk)]), 0.0)
        new_bond = (bond_ref[:, at(chunk)].astype(F32) + update).astype(BF16)
        new_bond_ref[:, at(chunk)] = new_bond
        bin_ref[2 * width :, at(chunk)] = new_bond

    def bond_message(chunk):
        out, fac_a, fac_c = gate_parts(dot(wm_half, bin_ref[:, at(chunk)]))
        up = up_ref[:, at(chunk)].astype(F32)
        dhid_ref[:width, at(chunk)] = (up * fac_a).astype(BF16)
        dhid_ref[width:, at(chunk)] = (up * fac_c).astype(BF16)
        dst_val[:width, at(chunk)] = out.astype(BF16)

    def bond_back(chunk):
        back = dot(wm_t, dhid_ref[:, at(chunk)])
        dtotal = bcot_ref[:, at(chunk)].astype(F32) + back[2 * width :]
        dtotal_ref[:, at(chunk)] = dtotal
        dlive_ref[:, at(chunk)] = jnp.where(live_bond(chunk), dtotal, 0.0).astype(BF16)
        source_val[:, at(chunk)] = back[:width].astype(BF16)
        dst_val[width:, at(chunk)] = back[width : 2 * width].astype(BF16)

    def summed_back(chunk):
        dsum = dot(wb_t, dlive_ref[:, at(chunk)]).astype(BF16)
        for k in range(CHUNK // GROUP):
            row = pl.multiple_of((chunk * (CHUNK // GROUP) + k) * width, width)
            dsum_ref[pl.ds(row, width), :] = dsum[:, k * GROUP : (k + 1) * GROUP]

    staged(bond_chunks, PER_B, update_bond, bond_message, bond_back, summed_back)

    def angle_up(chunk):
        got = dot(dsum_ref[...], table_pair[:, at(chunk)])
        up = pick_group(got, first_group(chunk), groups, width).astype(BF16)
        dz_ref[:width, at(chunk)] = up * fac_ref[:width, at(chunk)]
        dz_ref[width:, at(chunk)] = up * fac_ref[width:, at(chunk)]

    def angle_back(chunk):
        back = dot(wa_t[:width], dz_ref[:, at(chunk)])
        source_val[:, at(chunk, bonds)] = back.astype(BF16)

    far_rows = slice(atoms, atoms + slots)

    def back_and_far():
        from_dst, from_source = [], []

        def far_bond(chunk):
            from_dst.append(dot_nt(table_dst[far_rows, at(chunk)], dst_val[:, at(chunk)]))
            from_source.append(dot_nt(table_source[far_rows, at(chunk)], source_val[:, at(chunk)]))

        def far_angle(chunk):
            cols = at(chunk, bonds)
            from_source.append(dot_nt(table_source[far_rows, cols], source_val[:, cols]))

        def opening(chunk):
            angle_up(chunk)
            if chunk < bond_chunks:
                far_bond(chunk)

        skewed(angle_chunks, opening, angle_back, far_angle)
        for chunk in range(angle_chunks, bond_chunks):
            far_bond(chunk)
        both = sum(from_dst[1:], from_dst[0])
        single = sum(from_source[1:], from_source[0])
        far = jnp.concatenate([both[:, :width], both[:, width:] + single], 1)
        send2_ref[...] = far.reshape(send2_ref.shape).astype(BF16)

    region(back_and_far)

    def pooled_rows(rows):
        parts = [
            dot_nt(table_source[rows, :bonds], source_val[:, :bonds]),
            dot_nt(table_source[rows, bonds:], source_val[:, bonds:]),
        ]
        half = bonds // 2
        both = dot_nt(table_dst[rows, :half], dst_val[:, :half]) + dot_nt(
            table_dst[rows, half:], dst_val[:, half:]
        )
        return jnp.concatenate([both[:, :width], both[:, width:] + parts[0] + parts[1]], 1)

    start_all(send2_ref, recv2_ref, send_sem2, recv_sem2)
    recv2_ref[me] = send2_ref[me]

    def late_back(chunk):
        back_ref[:, at(chunk)] = dot(wa_t[width:], dz_ref[:, at(chunk)]).astype(BF16)

    def late(chunk):
        expand(back_ref[:width, at(chunk)], first_group(chunk), at(chunk))
        expand(back_ref[width:, at(chunk)], second_ref[:, at(chunk)] // GROUP, at(chunk, angles))

    def near_rows():
        kept_atom_ref[...] = atom_ref[...]
        kept_cot_ref[...] = acot_ref[...]
        kept_weight_ref[...] = wo_ref[...]
        near_ref[...] = pooled_rows(slice(0, atoms))

    region(near_rows)
    staged(angle_chunks, PER_L, late_back, late)

    def bond_grads():
        back = scatter(spread_ref, table_pair, 0, 2 * angles)
        for k in range(groups):
            cols = slice(k * GROUP, (k + 1) * GROUP)
            grad_bond_ref[:, cols] = (
                dtotal_ref[:, cols] + back[k * width : (k + 1) * width]
            ).astype(BF16)

    region(bond_grads)

    wait_all(send2_ref, recv2_ref, send_sem2, recv_sem2)
    returned = dot(table_list, recv2_ref[...].reshape(slots, 2 * width))
    total_ref[...] = near_ref[...] + returned


def local(n, *args):
    (atom_feat, bond_feat, angle_feat) = args[:3]
    width, atoms = atom_feat.shape
    bonds = bond_feat.shape[1]
    angles = angle_feat.shape[1]
    slots = args[9].shape[1]
    groups = bonds // GROUP
    space_cols = atoms + slots
    args = list(args)
    for at in (10, 11, 13, 14):
        args[at] = args[at].reshape(1, -1)
    args[7] = args[7].T
    args = args[:12] + args[13:15] + [args[12].reshape(1, -1), args[15].reshape(1, -1)]
    vm = pl.BlockSpec(memory_space=pltpu.VMEM)
    anywhere = pl.BlockSpec(memory_space=pl.ANY)
    part = slots // n
    exchange = pltpu.VMEM((n, part, 2 * width), BF16)
    shapes = (atom_feat.shape, bond_feat.shape, atom_feat.shape, bond_feat.shape)
    held = pl.pallas_call(
        functools.partial(kernel, n, "dom"),
        out_shape=(
            pltpu.VMEM((atoms, 2 * width), F32),
            pltpu.VMEM(bond_feat.shape, BF16),
            pltpu.VMEM(bond_feat.shape, BF16),
            pltpu.VMEM(atom_feat.shape, BF16),
            pltpu.VMEM(atom_feat.shape, BF16),
            pltpu.VMEM((width, width), BF16),
        ),
        in_specs=[anywhere] * INPUTS,
        out_specs=[vm] * OUTPUTS,
        scratch_shapes=[
            pltpu.VMEM(arg.shape, arg.dtype) for k, arg in enumerate(args) if k != 2
        ]
        + [
            pltpu.SemaphoreType.DMA((INPUTS,)),
            pltpu.VMEM((4 * width, angles), BF16),
            exchange,
            exchange,
            exchange,
            exchange,
            pltpu.VMEM((GROUP, 2 * angles), BF16),
            pltpu.VMEM((space_cols, bonds + angles), BF16),
            pltpu.VMEM((space_cols, bonds), BF16),
            pltpu.VMEM((groups * width + 2 * groups, GROUP), BF16),
            pltpu.VMEM((3 * width, bonds), BF16),
            pltpu.VMEM((width, bonds), BF16),
            pltpu.VMEM((2 * width, angles), BF16),
            pltpu.VMEM((groups * width, 2 * angles), BF16),
            pltpu.VMEM((width, bonds), BF16),
            pltpu.VMEM((2 * width, bonds), BF16),
            pltpu.VMEM((width, bonds), F32),
            pltpu.VMEM((width, bonds), BF16),
            pltpu.VMEM((groups * width, GROUP), BF16),
            pltpu.VMEM((2 * width, angles), BF16),
            pltpu.VMEM((width, bonds + angles), BF16),
            pltpu.VMEM((2 * width, bonds), BF16),
            pltpu.VMEM((2 * width, angles), BF16),
            pltpu.VMEM((atoms, 2 * width), F32),
            pltpu.VMEM((2 * width, angles), F32),
            pltpu.SemaphoreType.DMA,
            pltpu.SemaphoreType.DMA,
            pltpu.SemaphoreType.DMA,
            pltpu.SemaphoreType.DMA,
        ],
        compiler_params=pltpu.CompilerParams(collective_id=0, has_side_effects=True),
    )(*args)
    return pl.pallas_call(
        write_out,
        out_shape=tuple(jax.ShapeDtypeStruct(shape, BF16) for shape in shapes),
        in_specs=[vm] * OUTPUTS,
        out_specs=[pl.BlockSpec(memory_space=pl.ANY)] * 4,
        scratch_shapes=[
            pltpu.VMEM(atom_feat.shape, BF16),
            pltpu.VMEM(atom_feat.shape, BF16),
            pltpu.SemaphoreType.DMA((4,)),
        ],
    )(*(pltpu.with_memory_space_constraint(each, pltpu.VMEM) for each in held))


def write_out(
    total_ref,
    new_bond_ref,
    grad_bond_ref,
    atom_ref,
    cot_ref,
    weight_ref,
    new_atom_out,
    new_bond_out,
    grad_atom_out,
    grad_bond_out,
    new_atom_ref,
    grad_atom_ref,
    sems,
):
    pairs = (
        (new_bond_ref, new_bond_out),
        (grad_bond_ref, grad_bond_out),
        (grad_atom_ref, grad_atom_out),
        (new_atom_ref, new_atom_out),
    )
    copies = [pltpu.make_async_copy(*pair, sems.at[k]) for k, pair in enumerate(pairs)]
    width = atom_ref.shape[0]
    copies[0].start()
    copies[1].start()
    total = jnp.transpose(total_ref[...])
    grad_atom_ref[...] = (cot_ref[...].astype(F32) + total[width:]).astype(BF16)
    copies[2].start()
    new_atom_ref[...] = (
        atom_ref[...].astype(F32) + dot(weight_ref[...], total[:width].astype(BF16))
    ).astype(BF16)
    copies[3].start()
    for copy in copies:
        copy.wait()


def solution(mesh):
    return jax.shard_map(
        functools.partial(local, mesh.shape["dom"]),
        mesh=mesh,
        in_specs=(
            P("member", "dom"),
            P("member", "dom"),
            P("member", "dom"),
            P("member", "dom"),
            P("member", "dom"),
            P("member", None),
            P("member", None),
            P("member", None),
            P("member", None),
            P("dom", None),
            P("dom"),
            P("dom"),
            P(),
            P("dom"),
            P("dom"),
            P(),
        ),
        out_specs=(P("member", "dom"), P("member", "dom"), P("member", "dom"), P("member", "dom")),
        check_vma=False,
    )
```
